32 devices in a mesh: groups: 2 (over x), seq: 16 (over z, y, core).
Axes of the slice: x: 2, y: 2, z: 4, core: 2. Of those that a mesh axis runs over, the one named last changes fastest.
Arguments:
- activations: bfloat16 [512, 14336], P(('groups', 'seq')), parts along dimension 0, may hold values from -6 to 6
- out_grads: bfloat16 [512, 2048], P(('groups', 'seq')), parts along dimension 0, may hold values from -6 to 6
- query_ids: int32 [512], P(('groups', 'seq')), parts along dimension 0, may hold values from 0 to 2, never falling along the last dimension, each value on 1 to 128 neighbouring positions
- act_basis: bfloat16 [64, 224, 224], P('seq'), may hold values from -0.375 to 0.375
- grad_basis: bfloat16 [2048, 2048], P(None, 'seq'), may hold values from -0.125 to 0.125
- eigenvalues: float32 [2048, 14336], P(None, 'seq'), may hold values from 8 to 80
Outputs:
- precond: bfloat16 [6, 2048, 14336], P('groups', None, 'seq'), parts along dimension 0
The draws below stay inside these ranges and needn't reach their ends.
There are 2 independent parts, one for each index of `groups`. The reference program is written for one: setup_inputs(seed, part) draws one part's arguments, and reference() takes and returns one part's arrays. A program takes and returns all parts, laid end to end along the dimension named above; an argument that names none is the same for every part. Nothing has to cross between parts.
Inputs may be any that keep to these rules, and one draw needn't show every extreme that they name: `query_ids`: query ids never fall along the tokens; each of the 3 queries has at least one and at most 128 tokens.
All inputs are finite; a program needn't handle non-finite values.
Results may differ from the reference program's by a relative error of at most 0.006.
Values may be sent and summed in bfloat16 or wider, within the bound.
No kernel may reach another device: no remote copies, remote signals or barrier semaphores. Data moves between devices by JAX's collectives and lax.ppermute only.
A program may use at most 128 MiB of HBM per device.

```python
import math
import jax
import jax.numpy as jnp
import numpy as np

D = 2048
FF = 14336
FB = 224
QUERIES = 3
TOKENS = 256
BLOCKS = 64


def level_of(key, dims, shards, least, largest):
    factor_of, own = 1.0, jax.random.fold_in(key, 6)
    for position, shards_of in shards:
        steps = jnp.exp(jax.random.uniform(jax.random.fold_in(own, position), (shards_of,), jnp.float32, least / len(shards), largest / len(shards)))
        factor_of = factor_of * jnp.repeat(steps, dims[position] // shards_of).reshape([-1 if axis == position else 1 for axis in range(len(dims))])
    return factor_of


def profile(count, total, reach, slope):
    weights = [(1 << 20) // math.isqrt(standing ** slope) + 1 for standing in range(2, count + 1)]
    spare, given = total - reach - (count - 1), [1] * (count - 1)
    while spare > 0:
        free = [i for i in range(count - 1) if given[i] < reach]
        mass, remaining = sum([weights[i] for i in free]), spare
        for i in free:
            more = min(reach - given[i], max(1, remaining * weights[i] // mass), spare)
            given[i] = given[i] + more
            spare = spare - more
    return np.array([reach] + given)


def ragged(rng, amount, total, reach, skew):
    if amount == 2:
        one = jax.random.randint(rng, (), max(1, total - reach), min(reach, total - 1) + 1)
        return jnp.stack([one, total - one])
    tallies = jnp.asarray(profile(amount, total, reach, skew), jnp.int32)
    couples = (amount - 1) // 2
    donor, sink = tallies[1:1 + 2 * couples:2], tallies[2:2 + 2 * couples:2]
    room = jnp.minimum(donor - 1, reach - sink)
    passed = jax.random.randint(jax.random.fold_in(rng, 1), (couples,), 0, 1 << 20) % (room + 1)
    tallies = tallies.at[1:1 + 2 * couples:2].set(donor - passed).at[2:2 + 2 * couples:2].set(sink + passed)
    return tallies[jax.random.permutation(jax.random.fold_in(rng, 2), amount)]


def normal_values(rng, extent, spread, most, pieces=(), held_as=jnp.bfloat16):
    gain = level_of(rng, extent, pieces, -0.22, 0.18) if pieces else 1.0
    entries = jax.random.normal(rng, extent, jnp.float32) * spread * gain
    return jnp.minimum(jnp.maximum(entries, -most), most).astype(held_as)


def setup_inputs(seed: int = 0, part: int = 0) -> dict:
    seeds = jax.random.split(jax.random.key(seed), 7)
    part_splits = jax.random.split(jax.random.fold_in(seeds[6], part), 7)
    activations = normal_values(part_splits[0], (TOKENS, FF), 1.0, 6.0, ((0, 16),))
    out_grads = normal_values(part_splits[1], (TOKENS, D), 1.0, 6.0, ((0, 16),))
    query_ids = jnp.searchsorted(jnp.cumsum(ragged(part_splits[2], QUERIES, TOKENS, TOKENS // 2, 0)), jnp.arange(TOKENS), side="right").astype(jnp.int32)
    act_basis = normal_values(seeds[3], (BLOCKS, FB, FB), FB ** -0.5, 0.375, ((0, 16),))
    grad_basis = normal_values(seeds[4], (D, D), D ** -0.5, 0.125, ((1, 16),))
    eigenvalues = jnp.clip(jnp.exp(math.log(80.0) - 2.3025851 * jax.random.uniform(seeds[5], (D, FF), jnp.float32) ** level_of(seeds[5], (D, FF), ((1, 16),), -0.2, 0.2)), 8.0, 80.0)
    return dict(activations=activations, out_grads=out_grads, query_ids=query_ids, act_basis=act_basis, grad_basis=grad_basis, eigenvalues=eigenvalues)


def reference(activations, out_grads, query_ids, act_basis, grad_basis, eigenvalues):
    all_tokens = activations.shape[0]
    blocks = act_basis.shape[0]
    block_order = act_basis.shape[1]
    out_units = grad_basis.shape[0]
    basis_wide = act_basis.astype(jnp.float32)
    rotated_act = jnp.einsum("tbi,bik->tbk", activations.reshape(all_tokens, blocks, block_order).astype(jnp.float32), basis_wide)
    rotated_act = rotated_act.astype(jnp.bfloat16).reshape(all_tokens, blocks * block_order)
    rotated_grad = jnp.dot(out_grads, grad_basis, preferred_element_type=jnp.float32).astype(jnp.bfloat16)
    outputs = []
    for query_index in range(QUERIES):
        selected = jnp.where((query_ids == query_index)[:, None], rotated_act, jnp.zeros_like(rotated_act))
        moments = jnp.dot(rotated_grad.T, selected, preferred_element_type=jnp.float32)
        scaled = (moments / eigenvalues).astype(jnp.bfloat16)
        rotated_back = jnp.einsum("dbk,bik->dbi", scaled.reshape(out_units, blocks, block_order).astype(jnp.float32), basis_wide)
        rotated_back = rotated_back.astype(jnp.bfloat16).reshape(out_units, blocks * block_order)
        outputs.append(jnp.dot(grad_basis, rotated_back, preferred_element_type=jnp.float32).astype(jnp.bfloat16))
    return jnp.stack(outputs, axis=0)
```

```python
import functools

import jax
import jax.numpy as jnp
from jax import lax
from jax.experimental import pallas as pl
from jax.experimental.pallas import tpu as pltpu
from jax.sharding import Mesh
from jax.sharding import PartitionSpec as P

QUERIES = 3
LANES = 128
AXES = ("g", "z", "y", "c")


def windows(width, order):
    out = []
    for n0 in range(0, width, 2 * LANES):
        n1 = min(n0 + 2 * LANES, width)
        k0 = (n0 // order) * order // LANES * LANES
        k1 = min(width, -(-((n1 - 1) // order + 1) * order // LANES) * LANES)
        out.append((n0, n1, k0, k1))
    return out


def level_kernel(order, first, *refs):
    ids_ref = refs[0]
    og_ref, sel_ref, wt_ref = refs[1:4]
    basis_refs = refs[4:8]
    eig_refs = refs[8:12]
    if first:
        acc_ref = None
        out_ref, rb_ref = refs[12:]
    else:
        acc_ref, out_ref, rb_ref = refs[12:]
    del ids_ref
    step = pl.program_id(0)
    rows = out_ref.shape[1]
    width = out_ref.shape[2]
    shard = basis_refs[0].shape[1]

    @pl.when(step == 0)
    def _():
        for pair in range(2):
            basis = jnp.concatenate([r[...] for r in basis_refs[2 * pair : 2 * pair + 2]], axis=1)
            rg = jnp.dot(og_ref[...], basis, preferred_element_type=jnp.float32)
            rgt = rg.astype(jnp.bfloat16).T
            inv = 1.0 / jnp.concatenate([r[...] for r in eig_refs[2 * pair : 2 * pair + 2]], axis=0)
            for q in range(QUERIES):
                m = jnp.dot(rgt, sel_ref[q], preferred_element_type=jnp.float32)
                s = (m * inv).astype(jnp.bfloat16)
                for n0, n1, k0, k1 in windows(width, order):
                    back = jnp.dot(
                        s[:, k0:k1], wt_ref[k0:k1, n0:n1], preferred_element_type=jnp.float32
                    )
                    rb_ref[q, 2 * pair * shard : 2 * (pair + 1) * shard, n0:n1] = back.astype(
                        jnp.bfloat16
                    )

    at = pl.ds(pl.multiple_of(step * rows, rows), rows)
    lhs = jnp.concatenate([r[at, :] for r in basis_refs], axis=1)
    for q in range(QUERIES):
        part = jnp.dot(lhs, rb_ref[q], preferred_element_type=jnp.float32)
        if not first:
            part = part + acc_ref[q].astype(jnp.float32)
        out_ref[q] = part.astype(jnp.bfloat16)


def level(order, shard_ids, og, sel, wt, bases, eig, acc):
    units = og.shape[1]
    width = sel.shape[2]
    shard = bases[0].shape[1]
    rows = 2 * LANES
    first = acc is None
    const2 = lambda i, s: (0, 0)
    one = pl.Buffered(1)
    in_specs = [
        pl.BlockSpec(og.shape, const2, pipeline_mode=one),
        pl.BlockSpec(sel.shape, lambda i, s: (0, 0, 0), pipeline_mode=one),
        pl.BlockSpec(wt.shape, const2, pipeline_mode=one),
    ]
    in_specs += [pl.BlockSpec(bases[0].shape, const2, pipeline_mode=one)] * 4
    for j in range(4):
        in_specs.append(
            pl.BlockSpec((shard, width), lambda i, s, j=j: (s[j], 0), pipeline_mode=one)
        )
    out_block = pl.BlockSpec((QUERIES, rows, width), lambda i, s: (0, i, 0))
    args = [og, sel, wt, *bases, eig, eig, eig, eig]
    if not first:
        in_specs.append(out_block)
        args.append(acc)
    flops = 2 * QUERIES * width * 4 * shard * units
    return pl.pallas_call(
        functools.partial(level_kernel, order, first),
        out_shape=jax.ShapeDtypeStruct((QUERIES, units, width), jnp.bfloat16),
        grid_spec=pltpu.PrefetchScalarGridSpec(
            num_scalar_prefetch=1,
            grid=(units // rows,),
            in_specs=in_specs,
            out_specs=out_block,
            scratch_shapes=[pltpu.VMEM((QUERIES, 4 * shard, width), jnp.bfloat16)],
        ),
        input_output_aliases={} if first else {len(args): 0},
        compiler_params=pltpu.CompilerParams(
            dimension_semantics=("arbitrary",), vmem_limit_bytes=36 << 20
        ),
        cost_estimate=pl.CostEstimate(
            flops=flops, bytes_accessed=2 * QUERIES * units * width * 2, transcendentals=0
        ),
        name="level_first" if first else "level_next",
    )(shard_ids, *args)


def block_diagonal(blocks):
    count, order, _ = blocks.shape
    rows = [
        jnp.pad(blocks[b], ((0, 0), (b * order, (count - 1 - b) * order))) for b in range(count)
    ]
    return jnp.concatenate(rows, axis=0)


def ring_of(nz):
    return [0] + list(range(1, nz, 2)) + [z for z in range(nz - 1, 0, -1) if z % 2 == 0]


def streamed(shape, activations, out_grads, query_ids, act_basis, grad_basis, eigenvalues):
    ng, nz, ny, nc = shape
    count, order, _ = act_basis.shape
    width = count * order
    tokens = activations.shape[0]
    chips = nz * ny
    units = grad_basis.shape[0]

    def enc(g, z, y, c):
        return ((g * nz + z) * ny + y) * nc + c

    every = [
        (g, z, y, c) for g in range(ng) for z in range(nz) for y in range(ny) for c in range(nc)
    ]
    order_z = ring_of(nz)
    follow = {z: order_z[(i + 1) % nz] for i, z in enumerate(order_z)}
    before = {v: k for k, v in follow.items()}
    perm_core = [(enc(g, z, y, c), enc(g, z, y, 1 - c)) for g, z, y, c in every]
    perm_y = [(enc(g, z, y, c), enc(g, z, 1 - y, c)) for g, z, y, c in every]
    perm_z = [(enc(g, z, y, c), enc(g, follow[z], y, c)) for g, z, y, c in every]
    move = lambda v, p: lax.ppermute(v, AXES, p)

    ids = jnp.broadcast_to(query_ids.astype(jnp.bfloat16)[:, None], (tokens, LANES))
    common = jnp.concatenate([out_grads, ids], axis=1)
    parcels = jnp.concatenate(
        [
            activations.reshape(tokens, chips, nc * width).transpose(1, 0, 2),
            jnp.broadcast_to(common[None], (chips,) + common.shape),
        ],
        axis=2,
    )
    got = lax.all_to_all(parcels, ("z", "y"), split_axis=0, concat_axis=0, tiled=True)
    got = got.reshape(chips * tokens, nc * width + units + LANES)
    core = lax.axis_index("c")
    low, high, shared = got[:, :width], got[:, width : 2 * width], got[:, 2 * width :]
    mine = jnp.where(core == 0, low, high)
    other = jnp.where(core == 0, high, low)
    swapped = move(jnp.concatenate([other, shared], axis=1), perm_core)
    columns = jnp.concatenate([mine, swapped[:, :width]], axis=0)
    grads = jnp.concatenate([shared, swapped[:, width:]], axis=0)
    og, token_query = grads[:, :units], grads[:, units]

    levels = []
    own = grad_basis
    for k in range(nz):
        if k:
            own = move(own, perm_z)
        across = move(own, perm_y)
        levels.append((own, across, move(own, perm_core), move(across, perm_core)))

    rotated_act = jnp.dot(
        columns, block_diagonal(act_basis), preferred_element_type=jnp.float32
    ).astype(jnp.bfloat16)
    zero = jnp.zeros((), jnp.bfloat16)
    sel = jnp.stack(
        [
            jnp.where((token_query == jnp.bfloat16(q))[:, None], rotated_act, zero)
            for q in range(QUERIES)
        ]
    )
    wt = block_diagonal(jnp.swapaxes(act_basis, 1, 2))

    z, y, c = lax.axis_index("z"), lax.axis_index("y"), lax.axis_index("c")
    acc = None
    level_z = list(range(nz))
    for k in range(nz):
        zk = jnp.asarray(level_z, jnp.int32)[z]
        shard_ids = jnp.stack(
            [(zk * ny + yy) * nc + cc for cc in (c, 1 - c) for yy in (y, 1 - y)]
        ).astype(jnp.int32)
        acc = level(order, shard_ids, og, sel, wt, levels[k], eigenvalues, acc)
        level_z = [before[v] for v in level_z]
    return acc


def plain(activations, out_grads, query_ids, act_basis, grad_basis, eigenvalues):
    local_blocks, block_order = act_basis.shape[:2]
    out_units = grad_basis.shape[0]
    columns = lax.all_to_all(activations, AXES[1:], split_axis=1, concat_axis=0, tiled=True)
    all_tokens = columns.shape[0]
    local_width = local_blocks * block_order
    rotated_act = jnp.einsum(
        "tbi,bik->tbk",
        columns.reshape(all_tokens, local_blocks, block_order),
        act_basis,
        preferred_element_type=jnp.float32,
    )
    rotated_act = rotated_act.astype(jnp.bfloat16).reshape(all_tokens, local_width)
    full_basis = lax.all_gather(grad_basis, AXES[1:], axis=1, tiled=True)
    own_rotated = jnp.dot(out_grads, full_basis, preferred_element_type=jnp.float32).astype(
        jnp.bfloat16
    )
    rotated_grad = lax.all_gather(own_rotated, AXES[1:], axis=0, tiled=True)
    token_query = lax.all_gather(query_ids, AXES[1:], axis=0, tiled=True)
    selector = (token_query[:, None] == jnp.arange(QUERIES, dtype=jnp.int32)[None, :]).astype(
        jnp.bfloat16
    )
    results = []
    for q in range(QUERIES):
        moments = lax.dot_general(
            rotated_grad,
            rotated_act * selector[:, q : q + 1],
            (((0,), (0,)), ((), ())),
            preferred_element_type=jnp.float32,
        )
        scaled = (moments / eigenvalues).astype(jnp.bfloat16)
        back = jnp.einsum(
            "dbk,bik->dbi",
            scaled.reshape(out_units, local_blocks, block_order),
            act_basis,
            preferred_element_type=jnp.float32,
        )
        back = back.astype(jnp.bfloat16).reshape(out_units, local_width)
        results.append(
            jnp.dot(full_basis, back, preferred_element_type=jnp.float32).astype(jnp.bfloat16)
        )
    return jnp.stack(results, axis=0)


def solution(mesh):
    ng, ns = mesh.shape["groups"], mesh.shape["seq"]
    ny = nc = 2
    nz = ns // (ny * nc)
    shape = (ng, nz, ny, nc)
    fine = Mesh(mesh.devices.reshape(shape), AXES)
    seq = AXES[1:]

    def body(activations, out_grads, query_ids, act_basis, grad_basis, eigenvalues):
        shard = grad_basis.shape[1]
        width = act_basis.shape[0] * act_basis.shape[1]
        if shard % LANES or width % LANES or nz % 2:
            return plain(activations, out_grads, query_ids, act_basis, grad_basis, eigenvalues)
        return streamed(
            shape, activations, out_grads, query_ids, act_basis, grad_basis, eigenvalues
        )

    return jax.shard_map(
        body,
        mesh=fine,
        in_specs=(
            P(AXES, None),
            P(AXES, None),
            P(AXES),
            P(seq, None, None),
            P(None, seq),
            P(None, seq),
        ),
        out_specs=P("g", None, seq),
        check_vma=False,
    )
```

```python
import functools

import jax
import jax.numpy as jnp
from jax import lax
from jax.experimental import pallas as pl
from jax.experimental.pallas import tpu as pltpu
from jax.sharding import Mesh
from jax.sharding import PartitionSpec as P


QUERIES = 3
LANES = 128
ROWS = 256
AXES = ("g", "z", "y", "c")


def windows(width, order):
    out = []
    for n0 in range(0, width, 2 * LANES):
        n1 = min(n0 + 2 * LANES, width)
        k0 = (n0 // order) * order // LANES * LANES
        k1 = min(width, -(-((n1 - 1) // order + 1) * order // LANES) * LANES)
        out.append((n0, n1, k0, k1))
    return out


def basis_kernel(blocks_ref, dense_ref):
    count, order, _ = blocks_ref.shape
    dense_ref[...] = jnp.zeros_like(dense_ref)
    for b in range(count):
        dense_ref[b * order : (b + 1) * order, b * order : (b + 1) * order] = blocks_ref[b]


def block_diagonal(blocks):
    count, order, _ = blocks.shape
    return pl.pallas_call(
        basis_kernel,
        out_shape=jax.ShapeDtypeStruct((count * order,) * 2, blocks.dtype),
        compiler_params=pltpu.CompilerParams(vmem_limit_bytes=8 << 20),
        name="dense_basis",
    )(blocks)


def tokens_kernel(order, core_ref, got_ref, swap_ref, dense_ref, sel_ref, og_ref):
    half = got_ref.shape[0]
    units = og_ref.shape[1]
    width = dense_ref.shape[0]
    shared = got_ref.shape[1] - units - LANES
    at = pl.ds(pl.multiple_of(core_ref[0] * width, LANES), width)
    for i, ref in enumerate((got_ref, swap_ref)):
        rows = slice(i * half, (i + 1) * half)
        og_ref[rows, :] = ref[:, shared : shared + units]
        ids = ref[:, shared + units :][:, :1].astype(jnp.float32)
        columns = ref[:, at]
        for n0, n1, k0, k1 in windows(width, order):
            turned = jnp.dot(
                columns[:, k0:k1], dense_ref[k0:k1, n0:n1], preferred_element_type=jnp.float32
            )
            for q in range(QUERIES):
                sel_ref[q, rows, n0:n1] = jnp.where(ids == float(q), turned, 0.0).astype(
                    jnp.bfloat16
                )


def tokens_of(order, core, got, swapped, dense, units):
    half = got.shape[0]
    width = dense.shape[0]
    return pl.pallas_call(
        functools.partial(tokens_kernel, order),
        out_shape=(
            jax.ShapeDtypeStruct((QUERIES, 2 * half, width), jnp.bfloat16),
            jax.ShapeDtypeStruct((2 * half, units), jnp.bfloat16),
        ),
        in_specs=[
            pl.BlockSpec(memory_space=pltpu.SMEM),
            pl.BlockSpec(got.shape, lambda: (0, 0)),
            pl.BlockSpec(swapped.shape, lambda: (0, 0)),
            pl.BlockSpec(dense.shape, lambda: (0, 0)),
        ],
        out_specs=(
            pl.BlockSpec((QUERIES, 2 * half, width), lambda: (0, 0, 0)),
            pl.BlockSpec((2 * half, units), lambda: (0, 0)),
        ),
        compiler_params=pltpu.CompilerParams(vmem_limit_bytes=20 << 20),
        cost_estimate=pl.CostEstimate(
            flops=4 * half * width * width, bytes_accessed=4 << 20, transcendentals=0
        ),
        name="tokens",
    )(core, got, swapped, dense)


def half_kernel(order, first, count, *refs):
    ids_ref, og_ref, sel_ref, dense_ref = refs[:4]
    basis_refs = refs[4 : 4 + count]
    eig_ref = refs[4 + count]
    if first:
        acc_ref = None
        out_ref, rgt_ref, inv_ref, rb_ref, sems = refs[5 + count :]
    else:
        acc_ref, out_ref, rgt_ref, inv_ref, rb_ref, sems = refs[5 + count :]
    step = pl.program_id(0)
    rows, width = out_ref.shape[1:]
    shard = basis_refs[0].shape[1]

    @pl.when(step == 0)
    def _():
        def fetch(j):
            at = pl.ds(pl.multiple_of(ids_ref[j] * shard, shard), shard)
            to = pl.ds(pl.multiple_of(j * shard, shard), shard)
            return pltpu.make_async_copy(eig_ref.at[at, :], inv_ref.at[to, :], sems.at[j])

        for j in range(count):
            fetch(j).start()
        for j in range(0, count, 2):
            basis = jnp.concatenate([r[...] for r in basis_refs[j : j + 2]], axis=1)
            rg = jnp.dot(og_ref[...], basis, preferred_element_type=jnp.float32)
            rgt_ref[j * shard : (j + 2) * shard, :] = rg.astype(jnp.bfloat16).T

        @pl.loop(0, count // 2)
        def _(i):
            fetch(2 * i).wait()
            fetch(2 * i + 1).wait()
            at = pl.ds(pl.multiple_of(i * 2 * shard, 2 * shard), 2 * shard)
            inv = 1.0 / inv_ref[at, :]
            for q in range(QUERIES):
                m = jnp.dot(rgt_ref[at, :], sel_ref[q], preferred_element_type=jnp.float32)
                s = (m * inv).astype(jnp.bfloat16)
                for n0, n1, k0, k1 in windows(width, order):
                    back = lax.dot_general(
                        s[:, k0:k1],
                        dense_ref[n0:n1, k0:k1],
                        (((1,), (1,)), ((), ())),
                        preferred_element_type=jnp.float32,
                    )
                    rb_ref[at, q * width + n0 : q * width + n1] = back.astype(jnp.bfloat16)

    at = pl.ds(pl.multiple_of(step * rows, rows), rows)
    lhs = jnp.concatenate([r[at, :] for r in basis_refs], axis=1)
    part = jnp.dot(lhs, rb_ref[...], preferred_element_type=jnp.float32)
    for q in range(QUERIES):
        own = part[:, q * width : (q + 1) * width]
        if not first:
            own = own + acc_ref[q].astype(jnp.float32)
        out_ref[q] = own.astype(out_ref.dtype)


def half_of(order, shard_ids, og, sel, dense, bases, eig, acc):
    tokens, units = og.shape
    width = sel.shape[2]
    shard = bases[0].shape[1]
    count = len(bases)
    rows = min(units, ROWS)
    first = acc is None
    whole = pl.BlockSpec(memory_space=pltpu.VMEM)
    once = pl.Buffered(1)
    in_specs = [
        pl.BlockSpec(og.shape, lambda i, s: (0, 0), pipeline_mode=once),
        pl.BlockSpec(sel.shape, lambda i, s: (0, 0, 0), pipeline_mode=once),
        pl.BlockSpec(dense.shape, lambda i, s: (0, 0), pipeline_mode=once),
    ]
    in_specs += [whole] * count
    in_specs.append(pl.BlockSpec(memory_space=pltpu.HBM))
    out_block = pl.BlockSpec((QUERIES, rows, width), lambda i, s: (0, i, 0))
    args = [og, sel, dense, *bases, pltpu.with_memory_space_constraint(eig, pltpu.HBM)]
    if not first:
        in_specs.append(out_block)
        args.append(pltpu.with_memory_space_constraint(acc, pltpu.HBM))
    return pl.pallas_call(
        functools.partial(half_kernel, order, first, count),
        out_shape=pltpu.HBM((QUERIES, units, width), jnp.bfloat16),
        grid_spec=pltpu.PrefetchScalarGridSpec(
            num_scalar_prefetch=1,
            grid=(units // rows,),
            in_specs=in_specs,
            out_specs=out_block,
            scratch_shapes=[
                pltpu.VMEM((count * shard, tokens), jnp.bfloat16),
                pltpu.VMEM((count * shard, width), jnp.float32),
                pltpu.VMEM((count * shard, QUERIES * width), jnp.bfloat16),
                pltpu.SemaphoreType.DMA((count,)),
            ],
        ),
        compiler_params=pltpu.CompilerParams(
            dimension_semantics=("arbitrary",), vmem_limit_bytes=30 << 20
        ),
        cost_estimate=pl.CostEstimate(
            flops=2 * QUERIES * width * count * shard * units,
            bytes_accessed=QUERIES * units * width * (2 if first else 4),
            transcendentals=0,
        ),
        name="half_first" if first else "half_next",
    )(shard_ids, *args)


def ring_of(nz):
    return [0] + list(range(1, nz, 2)) + [z for z in range(nz - 1, 0, -1) if z % 2 == 0]


def streamed(shape, activations, out_grads, query_ids, act_basis, grad_basis, eigenvalues):
    ng, nz, ny, nc = shape
    count, order, _ = act_basis.shape
    width = count * order
    tokens = activations.shape[0]
    chips = nz * ny
    units = grad_basis.shape[0]

    def enc(g, z, y, c):
        return ((g * nz + z) * ny + y) * nc + c

    every = [
        (g, z, y, c) for g in range(ng) for z in range(nz) for y in range(ny) for c in range(nc)
    ]
    order_z = ring_of(nz)
    follow = {z: order_z[(i + 1) % nz] for i, z in enumerate(order_z)}
    before = {v: k for k, v in follow.items()}
    perm_core = [(enc(g, z, y, c), enc(g, z, y, 1 - c)) for g, z, y, c in every]
    perm_y = [(enc(g, z, y, c), enc(g, z, 1 - y, c)) for g, z, y, c in every]
    perm_z = [(enc(g, z, y, c), enc(g, follow[z], y, c)) for g, z, y, c in every]
    perm_zr = [(t, s) for s, t in perm_z]
    move = lambda v, p: lax.ppermute(v, AXES, p)

    ids = jnp.broadcast_to(query_ids.astype(jnp.bfloat16)[:, None], (tokens, LANES))
    common = jnp.concatenate([out_grads, ids], axis=1)
    parcels = jnp.concatenate(
        [
            activations.reshape(tokens, chips, nc * width).transpose(1, 0, 2),
            jnp.broadcast_to(common[None], (chips,) + common.shape),
        ],
        axis=2,
    )
    got = lax.all_to_all(parcels, ("z", "y"), split_axis=0, concat_axis=0, tiled=True)
    got = got.reshape(chips * tokens, nc * width + units + LANES)
    swapped = move(got, perm_core)

    along = [grad_basis] + [None] * (nz - 1)
    for k in range(1, nz // 2 + 1):
        along[k] = move(along[k - 1], perm_z)
        if nz - k > k:
            along[nz - k] = move(along[(nz - k + 1) % nz], perm_zr)
    levels = []
    for k in range(nz):
        across = move(along[k], perm_y)
        far = move(along[k], perm_core)
        far_across = move(across, perm_core)
        levels.append((along[k], across, far, far_across))

    z, y, c = lax.axis_index("z"), lax.axis_index("y"), lax.axis_index("c")
    dense = block_diagonal(act_basis)
    sel, og = tokens_of(
        order, c.astype(jnp.int32)[None], got, swapped, dense, units
    )

    ids_at, level_z = [], list(range(nz))
    for _ in range(nz):
        zk = sum(jnp.where(z == i, v, 0) for i, v in enumerate(level_z))
        ids_at.append([(zk * ny + yy) * nc + cc for cc in (c, 1 - c) for yy in (y, 1 - y)])
        level_z = [before[v] for v in level_z]
    acc = None
    for k in range(0, nz, nz // 2):
        span = range(k, k + nz // 2)
        shard_ids = jnp.stack([i for j in span for i in ids_at[j]]).astype(jnp.int32)
        bases = [b for j in span for b in levels[j]]
        acc = half_of(order, shard_ids, og, sel, dense, bases, eigenvalues, acc)
    return acc


def plain(activations, out_grads, query_ids, act_basis, grad_basis, eigenvalues):
    local_blocks, block_order = act_basis.shape[:2]
    out_units = grad_basis.shape[0]
    columns = lax.all_to_all(activations, AXES[1:], split_axis=1, concat_axis=0, tiled=True)
    all_tokens = columns.shape[0]
    local_width = local_blocks * block_order
    rotated_act = jnp.einsum(
        "tbi,bik->tbk",
        columns.reshape(all_tokens, local_blocks, block_order),
        act_basis,
        preferred_element_type=jnp.float32,
    )
    rotated_act = rotated_act.astype(jnp.bfloat16).reshape(all_tokens, local_width)
    full_basis = lax.all_gather(grad_basis, AXES[1:], axis=1, tiled=True)
    own_rotated = jnp.dot(out_grads, full_basis, preferred_element_type=jnp.float32).astype(
        jnp.bfloat16
    )
    rotated_grad = lax.all_gather(own_rotated, AXES[1:], axis=0, tiled=True)
    token_query = lax.all_gather(query_ids, AXES[1:], axis=0, tiled=True)
    selector = (token_query[:, None] == jnp.arange(QUERIES, dtype=jnp.int32)[None, :]).astype(
        jnp.bfloat16
    )
    results = []
    for q in range(QUERIES):
        moments = lax.dot_general(
            rotated_grad,
            rotated_act * selector[:, q : q + 1],
            (((0,), (0,)), ((), ())),
            preferred_element_type=jnp.float32,
        )
        scaled = (moments / eigenvalues).astype(jnp.bfloat16)
        back = jnp.einsum(
            "dbk,bik->dbi",
            scaled.reshape(out_units, local_blocks, block_order),
            act_basis,
            preferred_element_type=jnp.float32,
        )
        back = back.astype(jnp.bfloat16).reshape(out_units, local_width)
        results.append(
            jnp.dot(full_basis, back, preferred_element_type=jnp.float32).astype(jnp.bfloat16)
        )
    return jnp.stack(results, axis=0)


def solution(mesh):
    ng, ns = mesh.shape["groups"], mesh.shape["seq"]
    ny = nc = 2
    nz = ns // (ny * nc)
    shape = (ng, nz, ny, nc)
    fine = Mesh(mesh.devices.reshape(shape), AXES)
    seq = AXES[1:]

    def body(activations, out_grads, query_ids, act_basis, grad_basis, eigenvalues):
        shard = grad_basis.shape[1]
        width = act_basis.shape[0] * act_basis.shape[1]
        if shard % LANES or width % LANES or nz % 2:
            return plain(activations, out_grads, query_ids, act_basis, grad_basis, eigenvalues)
        return streamed(
            shape, activations, out_grads, query_ids, act_basis, grad_basis, eigenvalues
        )

    return jax.shard_map(
        body,
        mesh=fine,
        in_specs=(
            P(AXES, None),
            P(AXES, None),
            P(AXES),
            P(seq, None, None),
            P(None, seq),
            P(None, seq),
        ),
        out_specs=P("g", None, seq),
        check_vma=False,
    )
```

```python
import functools

import jax
import jax.numpy as jnp
from jax import lax
from jax.experimental import pallas as pl
from jax.experimental.pallas import tpu as pltpu
from jax.sharding import Mesh
from jax.sharding import PartitionSpec as P


QUERIES = 3
LANES = 128
ROWS = 256
AXES = ("g", "z", "y", "c")


def windows(width, order):
    out = []
    for n0 in range(0, width, 2 * LANES):
        n1 = min(n0 + 2 * LANES, width)
        k0 = (n0 // order) * order // LANES * LANES
        k1 = min(width, -(-((n1 - 1) // order + 1) * order // LANES) * LANES)
        out.append((n0, n1, k0, k1))
    return out


def basis_kernel(where_ref, blocks_ref, dense_ref):
    del where_ref
    count, order, _ = blocks_ref.shape
    dense_ref[...] = jnp.zeros_like(dense_ref)
    for b in range(count):
        dense_ref[b * order : (b + 1) * order, b * order : (b + 1) * order] = blocks_ref[b]


def block_diagonal(where, blocks):
    count, order, _ = blocks.shape
    return pl.pallas_call(
        basis_kernel,
        in_specs=[
            pl.BlockSpec(memory_space=pltpu.SMEM),
            pl.BlockSpec(blocks.shape, lambda: (0, 0, 0)),
        ],
        out_shape=jax.ShapeDtypeStruct((count * order,) * 2, blocks.dtype),
        compiler_params=pltpu.CompilerParams(vmem_limit_bytes=8 << 20),
        name="dense_basis",
    )(where, blocks)


def tokens_kernel(order, core_ref, got_ref, swap_ref, dense_ref, sel_ref, og_ref):
    half = got_ref.shape[0]
    units = og_ref.shape[1]
    width = dense_ref.shape[0]
    shared = got_ref.shape[1] - units - LANES
    at = pl.ds(pl.multiple_of(core_ref[2] * width, LANES), width)
    for i, ref in enumerate((got_ref, swap_ref)):
        rows = slice(i * half, (i + 1) * half)
        og_ref[rows, :] = ref[:, shared : shared + units]
        ids = ref[:, shared + units :][:, :1].astype(jnp.float32)
        columns = ref[:, at]
        for n0, n1, k0, k1 in windows(width, order):
            turned = jnp.dot(
                columns[:, k0:k1], dense_ref[k0:k1, n0:n1], preferred_element_type=jnp.float32
            )
            for q in range(QUERIES):
                sel_ref[q, rows, n0:n1] = jnp.where(ids == float(q), turned, 0.0).astype(
                    jnp.bfloat16
                )


def tokens_of(order, core, got, swapped, dense, units):
    half = got.shape[0]
    width = dense.shape[0]
    whole = pl.BlockSpec(memory_space=pltpu.VMEM)
    return pl.pallas_call(
        functools.partial(tokens_kernel, order),
        out_shape=(
            jax.ShapeDtypeStruct((QUERIES, 2 * half, width), jnp.bfloat16),
            jax.ShapeDtypeStruct((2 * half, units), jnp.bfloat16),
        ),
        in_specs=[pl.BlockSpec(memory_space=pltpu.SMEM), whole, whole, whole],
        out_specs=(whole, whole),
        compiler_params=pltpu.CompilerParams(vmem_limit_bytes=20 << 20),
        cost_estimate=pl.CostEstimate(
            flops=4 * half * width * width, bytes_accessed=4 << 20, transcendentals=0
        ),
        name="tokens",
    )(core, got, swapped, dense)


def half_kernel(order, first, count, sources, *refs):
    where_ref, og_ref, sel_ref, dense_ref = refs[:4]
    basis_refs = refs[4 : 4 + count]
    eig_ref = refs[4 + count]
    if first:
        acc_ref = None
        out_ref, rgt_ref, inv_ref, rb_ref, sems = refs[5 + count :]
    else:
        acc_ref, out_ref, rgt_ref, inv_ref, rb_ref, sems = refs[5 + count :]
    step = pl.program_id(0)
    rows, width = out_ref.shape[1:]
    shard = basis_refs[0].shape[1]

    @pl.when(step == 0)
    def _():
        z, y, c = where_ref[0], where_ref[1], where_ref[2]
        level_z = [
            sum(jnp.where(z == i, v, 0) for i, v in enumerate(table)) for table in sources
        ]

        def fetch(j):
            yy = y if j % 2 == 0 else 1 - y
            cc = c if j % 4 < 2 else 1 - c
            place = (level_z[j // 4] * 2 + yy) * 2 + cc
            at = pl.ds(pl.multiple_of(place * shard, shard), shard)
            to = pl.ds(pl.multiple_of(j * shard, shard), shard)
            return pltpu.make_async_copy(eig_ref.at[at, :], inv_ref.at[to, :], sems.at[j])

        fetches = [fetch(j) for j in range(count)]
        for f in fetches:
            f.start()
        for j in range(0, count, 2):
            basis = jnp.concatenate([r[...] for r in basis_refs[j : j + 2]], axis=1)
            rg = jnp.dot(og_ref[...], basis, preferred_element_type=jnp.float32)
            rgt_ref[j * shard : (j + 2) * shard, :] = rg.astype(jnp.bfloat16).T

        @pl.loop(0, count // 2)
        def _(i):
            for j in (2 * i, 2 * i + 1):
                to = pl.ds(pl.multiple_of(j * shard, shard), shard)
                pltpu.make_async_copy(
                    eig_ref.at[0:shard, :], inv_ref.at[to, :], sems.at[j]
                ).wait()
            at = pl.ds(pl.multiple_of(i * 2 * shard, 2 * shard), 2 * shard)
            inv = 1.0 / inv_ref[at, :]
            for q in range(QUERIES):
                m = jnp.dot(rgt_ref[at, :], sel_ref[q], preferred_element_type=jnp.float32)
                s = (m * inv).astype(jnp.bfloat16)
                for n0, n1, k0, k1 in windows(width, order):
                    back = lax.dot_general(
                        s[:, k0:k1],
                        dense_ref[n0:n1, k0:k1],
                        (((1,), (1,)), ((), ())),
                        preferred_element_type=jnp.float32,
                    )
                    rb_ref[at, q * width + n0 : q * width + n1] = back.astype(jnp.bfloat16)

    at = pl.ds(pl.multiple_of(step * rows, rows), rows)
    lhs = jnp.concatenate([r[at, :] for r in basis_refs], axis=1)
    part = jnp.dot(lhs, rb_ref[...], preferred_element_type=jnp.float32)
    for q in range(QUERIES):
        own = part[:, q * width : (q + 1) * width]
        if not first:
            own = own + acc_ref[q].astype(jnp.float32)
        out_ref[q] = own.astype(out_ref.dtype)


def half_of(order, sources, where, og, sel, dense, bases, eig, acc):
    tokens, units = og.shape
    width = sel.shape[2]
    shard = bases[0].shape[1]
    count = len(bases)
    rows = min(units, ROWS)
    first = acc is None
    whole = pl.BlockSpec(memory_space=pltpu.VMEM)
    in_specs = [whole] * 3
    in_specs += [whole] * count
    in_specs.append(pl.BlockSpec(memory_space=pltpu.HBM))
    out_block = pl.BlockSpec((QUERIES, rows, width), lambda i, s: (0, i, 0))
    args = [og, sel, dense, *bases, pltpu.with_memory_space_constraint(eig, pltpu.HBM)]
    if not first:
        in_specs.append(out_block)
        args.append(pltpu.with_memory_space_constraint(acc, pltpu.HBM))
    return pl.pallas_call(
        functools.partial(half_kernel, order, first, count, sources),
        out_shape=pltpu.HBM((QUERIES, units, width), jnp.bfloat16),
        grid_spec=pltpu.PrefetchScalarGridSpec(
            num_scalar_prefetch=1,
            grid=(units // rows,),
            in_specs=in_specs,
            out_specs=out_block,
            scratch_shapes=[
                pltpu.VMEM((count * shard, tokens), jnp.bfloat16),
                pltpu.VMEM((count * shard, width), jnp.float32),
                pltpu.VMEM((count * shard, QUERIES * width), jnp.bfloat16),
                pltpu.SemaphoreType.DMA((count,)),
            ],
        ),
        compiler_params=pltpu.CompilerParams(
            dimension_semantics=("arbitrary",), vmem_limit_bytes=30 << 20
        ),
        cost_estimate=pl.CostEstimate(
            flops=2 * QUERIES * width * count * shard * units,
            bytes_accessed=QUERIES * units * width * (2 if first else 4),
            transcendentals=0,
        ),
        name="half_first" if first else "half_next",
    )(where, *args)


def ring_of(nz):
    return [0] + list(range(1, nz, 2)) + [z for z in range(nz - 1, 0, -1) if z % 2 == 0]


def streamed(shape, activations, out_grads, query_ids, act_basis, grad_basis, eigenvalues):
    ng, nz, ny, nc = shape
    count, order, _ = act_basis.shape
    width = count * order
    tokens = activations.shape[0]
    chips = nz * ny
    units = grad_basis.shape[0]

    def enc(g, z, y, c):
        return ((g * nz + z) * ny + y) * nc + c

    every = [
        (g, z, y, c) for g in range(ng) for z in range(nz) for y in range(ny) for c in range(nc)
    ]
    order_z = ring_of(nz)
    follow = {z: order_z[(i + 1) % nz] for i, z in enumerate(order_z)}
    before = {v: k for k, v in follow.items()}
    perm_core = [(enc(g, z, y, c), enc(g, z, y, 1 - c)) for g, z, y, c in every]
    perm_y = [(enc(g, z, y, c), enc(g, z, 1 - y, c)) for g, z, y, c in every]
    perm_z = [(enc(g, z, y, c), enc(g, follow[z], y, c)) for g, z, y, c in every]
    perm_zr = [(t, s) for s, t in perm_z]
    move = lambda v, p: lax.ppermute(v, AXES, p)

    where = jnp.stack([lax.axis_index(a) for a in AXES[1:]]).astype(jnp.int32)

    ids = jnp.broadcast_to(query_ids.astype(jnp.bfloat16)[:, None], (tokens, LANES))
    common = jnp.concatenate([out_grads, ids], axis=1)
    parcels = jnp.concatenate(
        [
            activations.reshape(tokens, chips, nc * width).transpose(1, 0, 2),
            jnp.broadcast_to(common[None], (chips,) + common.shape),
        ],
        axis=2,
    )
    got = lax.all_to_all(parcels, ("z", "y"), split_axis=0, concat_axis=0, tiled=True)
    got = got.reshape(chips * tokens, nc * width + units + LANES)
    swapped = move(got, perm_core)

    along = [grad_basis] + [None] * (nz - 1)
    for k in range(1, nz // 2 + 1):
        along[k] = move(along[k - 1], perm_z)
        if nz - k > k:
            along[nz - k] = move(along[(nz - k + 1) % nz], perm_zr)
    levels = []
    for k in range(nz):
        across = move(along[k], perm_y)
        far = move(along[k], perm_core)
        far_across = move(across, perm_core)
        levels.append((along[k], across, far, far_across))

    dense = block_diagonal(where, act_basis)
    sel, og = tokens_of(order, where, got, swapped, dense, units)
    sources, level_z = [], list(range(nz))
    for _ in range(nz):
        sources.append(tuple(level_z))
        level_z = [before[v] for v in level_z]
    acc = None
    for k in range(0, nz, nz // 2):
        span = range(k, k + nz // 2)
        bases = [b for j in span for b in levels[j]]
        acc = half_of(
            order, [sources[j] for j in span], where, og, sel, dense, bases, eigenvalues, acc
        )
    return acc


def plain(activations, out_grads, query_ids, act_basis, grad_basis, eigenvalues):
    local_blocks, block_order = act_basis.shape[:2]
    out_units = grad_basis.shape[0]
    columns = lax.all_to_all(activations, AXES[1:], split_axis=1, concat_axis=0, tiled=True)
    all_tokens = columns.shape[0]
    local_width = local_blocks * block_order
    rotated_act = jnp.einsum(
        "tbi,bik->tbk",
        columns.reshape(all_tokens, local_blocks, block_order),
        act_basis,
        preferred_element_type=jnp.float32,
    )
    rotated_act = rotated_act.astype(jnp.bfloat16).reshape(all_tokens, local_width)
    full_basis = lax.all_gather(grad_basis, AXES[1:], axis=1, tiled=True)
    own_rotated = jnp.dot(out_grads, full_basis, preferred_element_type=jnp.float32).astype(
        jnp.bfloat16
    )
    rotated_grad = lax.all_gather(own_rotated, AXES[1:], axis=0, tiled=True)
    token_query = lax.all_gather(query_ids, AXES[1:], axis=0, tiled=True)
    selector = (token_query[:, None] == jnp.arange(QUERIES, dtype=jnp.int32)[None, :]).astype(
        jnp.bfloat16
    )
    results = []
    for q in range(QUERIES):
        moments = lax.dot_general(
            rotated_grad,
            rotated_act * selector[:, q : q + 1],
            (((0,), (0,)), ((), ())),
            preferred_element_type=jnp.float32,
        )
        scaled = (moments / eigenvalues).astype(jnp.bfloat16)
        back = jnp.einsum(
            "dbk,bik->dbi",
            scaled.reshape(out_units, local_blocks, block_order),
            act_basis,
            preferred_element_type=jnp.float32,
        )
        back = back.astype(jnp.bfloat16).reshape(out_units, local_width)
        results.append(
            jnp.dot(full_basis, back, preferred_element_type=jnp.float32).astype(jnp.bfloat16)
        )
    return jnp.stack(results, axis=0)


def solution(mesh):
    ng, ns = mesh.shape["groups"], mesh.shape["seq"]
    ny = nc = 2
    nz = ns // (ny * nc)
    shape = (ng, nz, ny, nc)
    fine = Mesh(mesh.devices.reshape(shape), AXES)
    seq = AXES[1:]

    def body(activations, out_grads, query_ids, act_basis, grad_basis, eigenvalues):
        shard = grad_basis.shape[1]
        width = act_basis.shape[0] * act_basis.shape[1]
        if shard % LANES or width % LANES or nz % 2:
            return plain(activations, out_grads, query_ids, act_basis, grad_basis, eigenvalues)
        return streamed(
            shape, activations, out_grads, query_ids, act_basis, grad_basis, eigenvalues
        )

    return jax.shard_map(
        body,
        mesh=fine,
        in_specs=(
            P(AXES, None),
            P(AXES, None),
            P(AXES),
            P(seq, None, None),
            P(None, seq),
            P(None, seq),
        ),
        out_specs=P("g", None, seq),
        check_vma=False,
    )
```

```python
import functools

import jax
import jax.numpy as jnp
from jax import lax
from jax.experimental import pallas as pl
from jax.experimental.pallas import tpu as pltpu
from jax.sharding import Mesh
from jax.sharding import PartitionSpec as P


QUERIES = 3
LANES = 128
ROWS = 256
AXES = ("g", "z", "y", "c")


def windows(width, order):
    out = []
    for n0 in range(0, width, 2 * LANES):
        n1 = min(n0 + 2 * LANES, width)
        k0 = (n0 // order) * order // LANES * LANES
        k1 = min(width, -(-((n1 - 1) // order + 1) * order // LANES) * LANES)
        out.append((n0, n1, k0, k1))
    return out


def basis_kernel(where_ref, blocks_ref, dense_ref):
    del where_ref
    count, order, _ = blocks_ref.shape
    dense_ref[...] = jnp.zeros_like(dense_ref)
    for b in range(count):
        dense_ref[b * order : (b + 1) * order, b * order : (b + 1) * order] = blocks_ref[b]


def block_diagonal(where, blocks):
    count, order, _ = blocks.shape
    return pl.pallas_call(
        basis_kernel,
        in_specs=[
            pl.BlockSpec(memory_space=pltpu.SMEM),
            pl.BlockSpec(blocks.shape, lambda: (0, 0, 0)),
        ],
        out_shape=jax.ShapeDtypeStruct((count * order,) * 2, blocks.dtype),
        compiler_params=pltpu.CompilerParams(vmem_limit_bytes=8 << 20),
        name="dense_basis",
    )(where, pltpu.with_memory_space_constraint(blocks, pltpu.HBM))


def tokens_kernel(order, core_ref, got_ref, swap_ref, dense_ref, sel_ref, og_ref):
    half = got_ref.shape[0]
    units = og_ref.shape[1]
    width = dense_ref.shape[0]
    shared = got_ref.shape[1] - units - LANES
    at = pl.ds(pl.multiple_of(core_ref[2] * width, LANES), width)
    for i, ref in enumerate((got_ref, swap_ref)):
        rows = slice(i * half, (i + 1) * half)
        og_ref[rows, :] = ref[:, shared : shared + units]
        ids = ref[:, shared + units :][:, :1].astype(jnp.float32)
        columns = ref[:, at]
        for n0, n1, k0, k1 in windows(width, order):
            turned = jnp.dot(
                columns[:, k0:k1], dense_ref[k0:k1, n0:n1], preferred_element_type=jnp.float32
            )
            for q in range(QUERIES):
                sel_ref[q, rows, n0:n1] = jnp.where(ids == float(q), turned, 0.0).astype(
                    jnp.bfloat16
                )


def tokens_of(order, core, got, swapped, dense, units):
    half = got.shape[0]
    width = dense.shape[0]
    whole = pl.BlockSpec(memory_space=pltpu.VMEM)
    return pl.pallas_call(
        functools.partial(tokens_kernel, order),
        out_shape=(
            jax.ShapeDtypeStruct((QUERIES, 2 * half, width), jnp.bfloat16),
            jax.ShapeDtypeStruct((2 * half, units), jnp.bfloat16),
        ),
        in_specs=[pl.BlockSpec(memory_space=pltpu.SMEM), whole, whole, whole],
        out_specs=(whole, whole),
        compiler_params=pltpu.CompilerParams(vmem_limit_bytes=20 << 20),
        cost_estimate=pl.CostEstimate(
            flops=4 * half * width * width, bytes_accessed=4 << 20, transcendentals=0
        ),
        name="tokens",
    )(core, got, swapped, dense)


def back_kernel(order, source, slot, *refs):
    where_ref, og_ref, sel_ref, dense_ref = refs[:4]
    basis_refs = refs[4:8]
    eig_ref = refs[8]
    rb_ref, rgt_ref, inv_ref, sems = refs[-4:]
    count = len(basis_refs)
    width = dense_ref.shape[0]
    shard = basis_refs[0].shape[1]
    z, y, c = where_ref[0], where_ref[1], where_ref[2]
    level_z = sum(jnp.where(z == i, v, 0) for i, v in enumerate(source))

    def fetch(j):
        yy = y if j % 2 == 0 else 1 - y
        cc = c if j % 4 < 2 else 1 - c
        place = (level_z * 2 + yy) * 2 + cc
        at = pl.ds(pl.multiple_of(place * shard, shard), shard)
        to = slice(j * shard, (j + 1) * shard)
        return pltpu.make_async_copy(eig_ref.at[at, :], inv_ref.at[to, :], sems.at[j])

    fetches = [fetch(j) for j in range(count)]
    for f in fetches:
        f.start()
    for j in range(0, count, 2):
        basis = jnp.concatenate([r[...] for r in basis_refs[j : j + 2]], axis=1)
        rg = jnp.dot(og_ref[...], basis, preferred_element_type=jnp.float32)
        rgt_ref[j * shard : (j + 2) * shard, :] = rg.astype(jnp.bfloat16).T
    for f in fetches:
        f.wait()

    @pl.loop(0, count // 2)
    def _(i):
        at = pl.ds(pl.multiple_of(i * 2 * shard, 2 * shard), 2 * shard)
        to = pl.ds(pl.multiple_of((slot * count + 2 * i) * shard, 2 * shard), 2 * shard)
        inv = 1.0 / inv_ref[at, :]
        for q in range(QUERIES):
            m = jnp.dot(rgt_ref[at, :], sel_ref[q], preferred_element_type=jnp.float32)
            s = (m * inv).astype(jnp.bfloat16)
            for n0, n1, k0, k1 in windows(width, order):
                back = lax.dot_general(
                    s[:, k0:k1],
                    dense_ref[n0:n1, k0:k1],
                    (((1,), (1,)), ((), ())),
                    preferred_element_type=jnp.float32,
                )
                rb_ref[to, q * width + n0 : q * width + n1] = back.astype(jnp.bfloat16)


def back_of(order, source, slot, slots, where, og, sel, dense, bases, eig, rb):
    tokens = og.shape[0]
    width = dense.shape[0]
    shard = bases[0].shape[1]
    count = len(bases)
    whole = pl.BlockSpec(memory_space=pltpu.VMEM)
    args = [og, sel, dense, *bases, pltpu.with_memory_space_constraint(eig, pltpu.HBM)]
    in_specs = [pl.BlockSpec(memory_space=pltpu.SMEM)] + [whole] * (3 + count)
    in_specs.append(pl.BlockSpec(memory_space=pltpu.HBM))
    if rb is not None:
        args.append(rb)
        in_specs.append(whole)
    return pl.pallas_call(
        functools.partial(back_kernel, order, source, slot),
        out_shape=jax.ShapeDtypeStruct((slots * count * shard, QUERIES * width), jnp.bfloat16),
        in_specs=in_specs,
        out_specs=whole,
        scratch_shapes=[
            pltpu.VMEM((count * shard, tokens), jnp.bfloat16),
            pltpu.VMEM((count * shard, width), jnp.float32),
            pltpu.SemaphoreType.DMA((count,)),
        ],
        input_output_aliases={} if rb is None else {len(args): 0},
        compiler_params=pltpu.CompilerParams(vmem_limit_bytes=10 << 20),
        cost_estimate=pl.CostEstimate(flops=5 << 30, bytes_accessed=4 << 20, transcendentals=0),
    )(where, *args)


def product_kernel(first, count, *refs):
    rb_ref = refs[0]
    basis_refs = refs[1 : 1 + count]
    acc_ref, out_ref = (None if first else refs[1 + count]), refs[-1]
    rows, width = out_ref.shape[1:]
    at = pl.ds(pl.multiple_of(pl.program_id(0) * rows, rows), rows)
    lhs = jnp.concatenate([r[at, :] for r in basis_refs], axis=1)
    part = jnp.dot(lhs, rb_ref[...], preferred_element_type=jnp.float32)
    for q in range(QUERIES):
        own = part[:, q * width : (q + 1) * width]
        if not first:
            own = own + acc_ref[q].astype(jnp.float32)
        out_ref[q] = own.astype(out_ref.dtype)


def product_of(rb, bases, acc):
    units, shard = bases[0].shape
    count = len(bases)
    width = rb.shape[1] // QUERIES
    rows = min(units, 2 * ROWS)
    first = acc is None
    whole = pl.BlockSpec(memory_space=pltpu.VMEM)
    out_block = pl.BlockSpec((QUERIES, rows, width), lambda i: (0, i, 0))
    in_specs = [whole] * (1 + count)
    args = [rb, *bases]
    if not first:
        in_specs.append(out_block)
        args.append(pltpu.with_memory_space_constraint(acc, pltpu.HBM))
    return pl.pallas_call(
        functools.partial(product_kernel, first, count),
        out_shape=pltpu.HBM((QUERIES, units, width), jnp.bfloat16),
        grid=(units // rows,),
        in_specs=in_specs,
        out_specs=out_block,
        compiler_params=pltpu.CompilerParams(
            dimension_semantics=("arbitrary",), vmem_limit_bytes=24 << 20
        ),
        cost_estimate=pl.CostEstimate(
            flops=2 * QUERIES * width * count * shard * units,
            bytes_accessed=QUERIES * units * width * (2 if first else 4),
            transcendentals=0,
        ),
    )(*args)


def half_kernel(order, first, count, sources, *refs):
    where_ref, og_ref, sel_ref, dense_ref = refs[:4]
    basis_refs = refs[4 : 4 + count]
    eig_ref = refs[4 + count]
    if first:
        acc_ref = None
        out_ref, rgt_ref, inv_ref, rb_ref, sems = refs[5 + count :]
    else:
        acc_ref, out_ref, rgt_ref, inv_ref, rb_ref, sems = refs[5 + count :]
    step = pl.program_id(0)
    rows, width = out_ref.shape[1:]
    shard = basis_refs[0].shape[1]

    @pl.when(step == 0)
    def _():
        z, y, c = where_ref[0], where_ref[1], where_ref[2]
        level_z = [
            sum(jnp.where(z == i, v, 0) for i, v in enumerate(table)) for table in sources
        ]

        def fetch(j):
            yy = y if j % 2 == 0 else 1 - y
            cc = c if j % 4 < 2 else 1 - c
            place = (level_z[j // 4] * 2 + yy) * 2 + cc
            at = pl.ds(pl.multiple_of(place * shard, shard), shard)
            to = pl.ds(pl.multiple_of(j * shard, shard), shard)
            return pltpu.make_async_copy(eig_ref.at[at, :], inv_ref.at[to, :], sems.at[j])

        fetches = [fetch(j) for j in range(count)]
        for f in fetches:
            f.start()
        for j in range(0, count, 2):
            basis = jnp.concatenate([r[...] for r in basis_refs[j : j + 2]], axis=1)
            rg = jnp.dot(og_ref[...], basis, preferred_element_type=jnp.float32)
            rgt_ref[j * shard : (j + 2) * shard, :] = rg.astype(jnp.bfloat16).T

        @pl.loop(0, count // 2)
        def _(i):
            for j in (2 * i, 2 * i + 1):
                to = pl.ds(pl.multiple_of(j * shard, shard), shard)
                pltpu.make_async_copy(
                    eig_ref.at[0:shard, :], inv_ref.at[to, :], sems.at[j]
                ).wait()
            at = pl.ds(pl.multiple_of(i * 2 * shard, 2 * shard), 2 * shard)
            inv = 1.0 / inv_ref[at, :]
            for q in range(QUERIES):
                m = jnp.dot(rgt_ref[at, :], sel_ref[q], preferred_element_type=jnp.float32)
                s = (m * inv).astype(jnp.bfloat16)
                for n0, n1, k0, k1 in windows(width, order):
                    back = lax.dot_general(
                        s[:, k0:k1],
                        dense_ref[n0:n1, k0:k1],
                        (((1,), (1,)), ((), ())),
                        preferred_element_type=jnp.float32,
                    )
                    rb_ref[at, q * width + n0 : q * width + n1] = back.astype(jnp.bfloat16)

    at = pl.ds(pl.multiple_of(step * rows, rows), rows)
    lhs = jnp.concatenate([r[at, :] for r in basis_refs], axis=1)
    part = jnp.dot(lhs, rb_ref[...], preferred_element_type=jnp.float32)
    for q in range(QUERIES):
        own = part[:, q * width : (q + 1) * width]
        if not first:
            own = own + acc_ref[q].astype(jnp.float32)
        out_ref[q] = own.astype(out_ref.dtype)


def half_of(order, sources, where, og, sel, dense, bases, eig, acc):
    tokens, units = og.shape
    width = sel.shape[2]
    shard = bases[0].shape[1]
    count = len(bases)
    rows = min(units, ROWS)
    first = acc is None
    whole = pl.BlockSpec(memory_space=pltpu.VMEM)
    in_specs = [whole] * 3
    in_specs += [whole] * count
    in_specs.append(pl.BlockSpec(memory_space=pltpu.HBM))
    out_block = pl.BlockSpec((QUERIES, rows, width), lambda i, s: (0, i, 0))
    args = [og, sel, dense, *bases, pltpu.with_memory_space_constraint(eig, pltpu.HBM)]
    if not first:
        in_specs.append(out_block)
        args.append(pltpu.with_memory_space_constraint(acc, pltpu.HBM))
    return pl.pallas_call(
        functools.partial(half_kernel, order, first, count, sources),
        out_shape=pltpu.HBM((QUERIES, units, width), jnp.bfloat16),
        grid_spec=pltpu.PrefetchScalarGridSpec(
            num_scalar_prefetch=1,
            grid=(units // rows,),
            in_specs=in_specs,
            out_specs=out_block,
            scratch_shapes=[
                pltpu.VMEM((count * shard, tokens), jnp.bfloat16),
                pltpu.VMEM((count * shard, width), jnp.float32),
                pltpu.VMEM((count * shard, QUERIES * width), jnp.bfloat16),
                pltpu.SemaphoreType.DMA((count,)),
            ],
        ),
        compiler_params=pltpu.CompilerParams(
            dimension_semantics=("arbitrary",), vmem_limit_bytes=30 << 20
        ),
        cost_estimate=pl.CostEstimate(
            flops=2 * QUERIES * width * count * shard * units,
            bytes_accessed=QUERIES * units * width * (2 if first else 4),
            transcendentals=0,
        ),
        name="half_first" if first else "half_next",
    )(where, *args)


def parcel_kernel(ids_ref, act_ref, grads_ref, out_ref):
    chips, tokens, _ = out_ref.shape
    units = grads_ref.shape[1]
    wide = act_ref.shape[1] // chips
    row = lax.broadcasted_iota(jnp.int32, (tokens, LANES), 0)
    ids = jnp.zeros((tokens, LANES), jnp.float32)
    for t in range(tokens):
        ids = jnp.where(row == t, ids_ref[t].astype(jnp.float32), ids)
    ids = ids.astype(jnp.bfloat16)
    for j in range(chips):
        out_ref[j, :, :wide] = act_ref[:, j * wide : (j + 1) * wide]
        out_ref[j, :, wide : wide + units] = grads_ref[...]
        out_ref[j, :, wide + units :] = ids


def parcels_of(chips, activations, out_grads, query_ids):
    tokens, units = out_grads.shape
    wide = activations.shape[1] // chips
    return pl.pallas_call(
        parcel_kernel,
        out_shape=jax.ShapeDtypeStruct((chips, tokens, wide + units + LANES), jnp.bfloat16),
        in_specs=[
            pl.BlockSpec(memory_space=pltpu.SMEM),
            pl.BlockSpec(activations.shape, lambda: (0, 0)),
            pl.BlockSpec(out_grads.shape, lambda: (0, 0)),
        ],
        out_specs=pl.BlockSpec((chips, tokens, wide + units + LANES), lambda: (0, 0, 0)),
        compiler_params=pltpu.CompilerParams(vmem_limit_bytes=8 << 20),
        name="parcels",
    )(query_ids, *(pltpu.with_memory_space_constraint(v, pltpu.HBM) for v in (activations, out_grads)))


def ring_of(nz):
    return [0] + list(range(1, nz, 2)) + [z for z in range(nz - 1, 0, -1) if z % 2 == 0]


def streamed(shape, activations, out_grads, query_ids, act_basis, grad_basis, eigenvalues):
    ng, nz, ny, nc = shape
    count, order, _ = act_basis.shape
    width = count * order
    tokens = activations.shape[0]
    chips = nz * ny
    units = grad_basis.shape[0]

    def enc(g, z, y, c):
        return ((g * nz + z) * ny + y) * nc + c

    every = [
        (g, z, y, c) for g in range(ng) for z in range(nz) for y in range(ny) for c in range(nc)
    ]
    order_z = ring_of(nz)
    follow = {z: order_z[(i + 1) % nz] for i, z in enumerate(order_z)}
    before = {v: k for k, v in follow.items()}
    perm_core = [(enc(g, z, y, c), enc(g, z, y, 1 - c)) for g, z, y, c in every]
    perm_y = [(enc(g, z, y, c), enc(g, z, 1 - y, c)) for g, z, y, c in every]
    perm_z = [(enc(g, z, y, c), enc(g, follow[z], y, c)) for g, z, y, c in every]
    perm_zr = [(t, s) for s, t in perm_z]
    move = lambda v, p: lax.ppermute(v, AXES, p)

    where = jnp.stack([lax.axis_index(a) for a in AXES[1:]]).astype(jnp.int32)

    parcels = parcels_of(chips, activations, out_grads, query_ids)
    got = lax.all_to_all(parcels, ("z", "y"), split_axis=0, concat_axis=0, tiled=True)
    got = got.reshape(chips * tokens, nc * width + units + LANES)
    swapped = move(got, perm_core)

    along = [grad_basis] + [None] * (nz - 1)
    for k in range(1, nz // 2 + 1):
        along[k] = move(along[k - 1], perm_z)
        if nz - k > k:
            along[nz - k] = move(along[(nz - k + 1) % nz], perm_zr)
    levels = []
    for k in range(nz):
        across = move(along[k], perm_y)
        far = move(along[k], perm_core)
        far_across = move(across, perm_core)
        levels.append((along[k], across, far, far_across))

    dense = block_diagonal(where, act_basis)
    sel, og = tokens_of(order, where, got, swapped, dense, units)
    sources, level_z = [], list(range(nz))
    for _ in range(nz):
        sources.append(tuple(level_z))
        level_z = [before[v] for v in level_z]
    slots = nz // 2
    rb = None
    for k in range(slots):
        rb = back_of(order, sources[k], k, slots, where, og, sel, dense, levels[k], eigenvalues, rb)
    acc = product_of(rb, [b for k in range(slots) for b in levels[k]], None)
    rest = range(slots, nz)
    bases = [b for k in rest for b in levels[k]]
    return half_of(
        order, [sources[k] for k in rest], where, og, sel, dense, bases, eigenvalues, acc
    )


def plain(activations, out_grads, query_ids, act_basis, grad_basis, eigenvalues):
    local_blocks, block_order = act_basis.shape[:2]
    out_units = grad_basis.shape[0]
    columns = lax.all_to_all(activations, AXES[1:], split_axis=1, concat_axis=0, tiled=True)
    all_tokens = columns.shape[0]
    local_width = local_blocks * block_order
    rotated_act = jnp.einsum(
        "tbi,bik->tbk",
        columns.reshape(all_tokens, local_blocks, block_order),
        act_basis,
        preferred_element_type=jnp.float32,
    )
    rotated_act = rotated_act.astype(jnp.bfloat16).reshape(all_tokens, local_width)
    full_basis = lax.all_gather(grad_basis, AXES[1:], axis=1, tiled=True)
    own_rotated = jnp.dot(out_grads, full_basis, preferred_element_type=jnp.float32).astype(
        jnp.bfloat16
    )
    rotated_grad = lax.all_gather(own_rotated, AXES[1:], axis=0, tiled=True)
    token_query = lax.all_gather(query_ids, AXES[1:], axis=0, tiled=True)
    selector = (token_query[:, None] == jnp.arange(QUERIES, dtype=jnp.int32)[None, :]).astype(
        jnp.bfloat16
    )
    results = []
    for q in range(QUERIES):
        moments = lax.dot_general(
            rotated_grad,
            rotated_act * selector[:, q : q + 1],
            (((0,), (0,)), ((), ())),
            preferred_element_type=jnp.float32,
        )
        scaled = (moments / eigenvalues).astype(jnp.bfloat16)
        back = jnp.einsum(
            "dbk,bik->dbi",
            scaled.reshape(out_units, local_blocks, block_order),
            act_basis,
            preferred_element_type=jnp.float32,
        )
        back = back.astype(jnp.bfloat16).reshape(out_units, local_width)
        results.append(
            jnp.dot(full_basis, back, preferred_element_type=jnp.float32).astype(jnp.bfloat16)
        )
    return jnp.stack(results, axis=0)


def solution(mesh):
    ng, ns = mesh.shape["groups"], mesh.shape["seq"]
    ny = nc = 2
    nz = ns // (ny * nc)
    shape = (ng, nz, ny, nc)
    fine = Mesh(mesh.devices.reshape(shape), AXES)
    seq = AXES[1:]

    def body(activations, out_grads, query_ids, act_basis, grad_basis, eigenvalues):
        shard = grad_basis.shape[1]
        width = act_basis.shape[0] * act_basis.shape[1]
        if shard % LANES or width % LANES or nz % 2:
            return plain(activations, out_grads, query_ids, act_basis, grad_basis, eigenvalues)
        return streamed(
            shape, activations, out_grads, query_ids, act_basis, grad_basis, eigenvalues
        )

    return jax.shard_map(
        body,
        mesh=fine,
        in_specs=(
            P(AXES, None),
            P(AXES, None),
            P(AXES),
            P(seq, None, None),
            P(None, seq),
            P(None, seq),
        ),
        out_specs=P("g", None, seq),
        check_vma=False,
    )
```

```python
import functools

import jax
import jax.numpy as jnp
from jax import lax
from jax.experimental import pallas as pl
from jax.experimental.pallas import tpu as pltpu
from jax.sharding import Mesh
from jax.sharding import PartitionSpec as P


QUERIES = 3
LANES = 128
ROWS = 256
AXES = ("g", "z", "y", "c")


def windows(width, order):
    out = []
    for n0 in range(0, width, 2 * LANES):
        n1 = min(n0 + 2 * LANES, width)
        k0 = (n0 // order) * order // LANES * LANES
        k1 = min(width, -(-((n1 - 1) // order + 1) * order // LANES) * LANES)
        out.append((n0, n1, k0, k1))
    return out


def basis_kernel(where_ref, blocks_ref, dense_ref):
    del where_ref
    count, order, _ = blocks_ref.shape
    dense_ref[...] = jnp.zeros_like(dense_ref)
    for b in range(count):
        dense_ref[b * order : (b + 1) * order, b * order : (b + 1) * order] = blocks_ref[b]


def block_diagonal(where, blocks):
    count, order, _ = blocks.shape
    return pl.pallas_call(
        basis_kernel,
        in_specs=[
            pl.BlockSpec(memory_space=pltpu.SMEM),
            pl.BlockSpec(blocks.shape, lambda: (0, 0, 0)),
        ],
        out_shape=jax.ShapeDtypeStruct((count * order,) * 2, blocks.dtype),
        compiler_params=pltpu.CompilerParams(vmem_limit_bytes=8 << 20),
        name="dense_basis",
    )(where, pltpu.with_memory_space_constraint(blocks, pltpu.HBM))


def tokens_kernel(order, core_ref, got_ref, swap_ref, dense_ref, sel_ref, og_ref):
    half = got_ref.shape[0]
    units = og_ref.shape[1]
    width = dense_ref.shape[0]
    shared = got_ref.shape[1] - units - LANES
    at = pl.ds(pl.multiple_of(core_ref[2] * width, LANES), width)
    for i, ref in enumerate((got_ref, swap_ref)):
        rows = slice(i * half, (i + 1) * half)
        og_ref[rows, :] = ref[:, shared : shared + units]
        ids = ref[:, shared + units :][:, :1].astype(jnp.float32)
        columns = ref[:, at]
        for n0, n1, k0, k1 in windows(width, order):
            turned = jnp.dot(
                columns[:, k0:k1], dense_ref[k0:k1, n0:n1], preferred_element_type=jnp.float32
            )
            for q in range(QUERIES):
                sel_ref[q, rows, n0:n1] = jnp.where(ids == float(q), turned, 0.0).astype(
                    jnp.bfloat16
                )


def tokens_of(order, core, got, swapped, dense, units):
    half = got.shape[0]
    width = dense.shape[0]
    whole = pl.BlockSpec(memory_space=pltpu.VMEM)
    return pl.pallas_call(
        functools.partial(tokens_kernel, order),
        out_shape=(
            jax.ShapeDtypeStruct((QUERIES, 2 * half, width), jnp.bfloat16),
            jax.ShapeDtypeStruct((2 * half, units), jnp.bfloat16),
        ),
        in_specs=[pl.BlockSpec(memory_space=pltpu.SMEM), whole, whole, whole],
        out_specs=(whole, whole),
        compiler_params=pltpu.CompilerParams(vmem_limit_bytes=20 << 20),
        cost_estimate=pl.CostEstimate(
            flops=4 * half * width * width, bytes_accessed=4 << 20, transcendentals=0
        ),
        name="tokens",
    )(core, got, swapped, dense)


def back_kernel(order, source, slot, *refs):
    where_ref, og_ref, sel_ref, dense_ref = refs[:4]
    basis_refs = refs[4:8]
    eig_ref = refs[8]
    rb_ref, rgt_ref, inv_ref, sems = refs[-4:]
    count = len(basis_refs)
    width = dense_ref.shape[0]
    shard = basis_refs[0].shape[1]
    z, y, c = where_ref[0], where_ref[1], where_ref[2]
    level_z = sum(jnp.where(z == i, v, 0) for i, v in enumerate(source))

    def fetch(j):
        yy = y if j % 2 == 0 else 1 - y
        cc = c if j % 4 < 2 else 1 - c
        place = (level_z * 2 + yy) * 2 + cc
        at = pl.ds(pl.multiple_of(place * shard, shard), shard)
        to = slice(j * shard, (j + 1) * shard)
        return pltpu.make_async_copy(eig_ref.at[at, :], inv_ref.at[to, :], sems.at[j])

    fetches = [fetch(j) for j in range(count)]
    for f in fetches:
        f.start()
    for j in range(0, count, 2):
        basis = jnp.concatenate([r[...] for r in basis_refs[j : j + 2]], axis=1)
        rg = jnp.dot(og_ref[...], basis, preferred_element_type=jnp.float32)
        rgt_ref[j * shard : (j + 2) * shard, :] = rg.astype(jnp.bfloat16).T
    for f in fetches:
        f.wait()

    @pl.loop(0, count // 2)
    def _(i):
        at = pl.ds(pl.multiple_of(i * 2 * shard, 2 * shard), 2 * shard)
        to = pl.ds(pl.multiple_of((slot * count + 2 * i) * shard, 2 * shard), 2 * shard)
        inv = 1.0 / inv_ref[at, :]
        for q in range(QUERIES):
            m = jnp.dot(rgt_ref[at, :], sel_ref[q], preferred_element_type=jnp.float32)
            s = (m * inv).astype(jnp.bfloat16)
            for n0, n1, k0, k1 in windows(width, order):
                back = lax.dot_general(
                    s[:, k0:k1],
                    dense_ref[n0:n1, k0:k1],
                    (((1,), (1,)), ((), ())),
                    preferred_element_type=jnp.float32,
                )
                rb_ref[to, q * width + n0 : q * width + n1] = back.astype(jnp.bfloat16)


def back_of(order, source, slot, slots, where, og, sel, dense, bases, eig, rb):
    tokens = og.shape[0]
    width = dense.shape[0]
    shard = bases[0].shape[1]
    count = len(bases)
    whole = pl.BlockSpec(memory_space=pltpu.VMEM)
    args = [og, sel, dense, *bases, pltpu.with_memory_space_constraint(eig, pltpu.HBM)]
    in_specs = [pl.BlockSpec(memory_space=pltpu.SMEM)] + [whole] * (3 + count)
    in_specs.append(pl.BlockSpec(memory_space=pltpu.HBM))
    if rb is not None:
        args.append(rb)
        in_specs.append(whole)
    return pl.pallas_call(
        functools.partial(back_kernel, order, source, slot),
        out_shape=jax.ShapeDtypeStruct((slots * count * shard, QUERIES * width), jnp.bfloat16),
        in_specs=in_specs,
        out_specs=whole,
        scratch_shapes=[
            pltpu.VMEM((count * shard, tokens), jnp.bfloat16),
            pltpu.VMEM((count * shard, width), jnp.float32),
            pltpu.SemaphoreType.DMA((count,)),
        ],
        input_output_aliases={} if rb is None else {len(args): 0},
        compiler_params=pltpu.CompilerParams(vmem_limit_bytes=10 << 20),
        cost_estimate=pl.CostEstimate(flops=5 << 30, bytes_accessed=4 << 20, transcendentals=0),
    )(where, *args)


def product_kernel(first, count, start, *refs):
    rb_ref = refs[0]
    basis_refs = refs[1 : 1 + count]
    acc_ref, out_ref = (None if first else refs[1 + count]), refs[-1]
    rows, width = out_ref.shape[1:]
    at = pl.ds(pl.multiple_of((pl.program_id(0) + start) * rows, rows), rows)
    lhs = jnp.concatenate([r[at, :] for r in basis_refs], axis=1)
    part = jnp.dot(lhs, rb_ref[...], preferred_element_type=jnp.float32)
    for q in range(QUERIES):
        own = part[:, q * width : (q + 1) * width]
        if not first:
            own = own + acc_ref[q].astype(jnp.float32)
        out_ref[q] = own.astype(out_ref.dtype)


def product_of(rb, bases, acc, start, steps, prior):
    units, shard = bases[0].shape
    count = len(bases)
    width = rb.shape[1] // QUERIES
    first = acc is None
    rows = min(units, ROWS if first else 2 * ROWS)
    whole = pl.BlockSpec(memory_space=pltpu.VMEM)
    out_block = pl.BlockSpec((QUERIES, rows, width), lambda i: (0, i + start, 0))
    in_specs = [whole] * (1 + count)
    args = [rb, *bases]
    if not first:
        in_specs.append(out_block)
        args.append(pltpu.with_memory_space_constraint(acc, pltpu.HBM))
    if prior is not None:
        in_specs.append(pl.BlockSpec(memory_space=pltpu.HBM))
        args.append(prior)
    return pl.pallas_call(
        functools.partial(product_kernel, first, count, start),
        out_shape=pltpu.HBM((QUERIES, units, width), jnp.bfloat16),
        grid=(steps,),
        in_specs=in_specs,
        out_specs=out_block,
        compiler_params=pltpu.CompilerParams(
            dimension_semantics=("arbitrary",), vmem_limit_bytes=24 << 20
        ),
        cost_estimate=pl.CostEstimate(
            flops=2 * QUERIES * width * count * shard * units,
            bytes_accessed=QUERIES * units * width * (2 if first else 4),
            transcendentals=0,
        ),
        input_output_aliases={} if prior is None else {len(args) - 1: 0},
    )(*args)


def parcel_kernel(ids_ref, act_ref, grads_ref, out_ref):
    chips, tokens, _ = out_ref.shape
    units = grads_ref.shape[1]
    wide = act_ref.shape[1] // chips
    row = lax.broadcasted_iota(jnp.int32, (tokens, LANES), 0)
    ids = jnp.zeros((tokens, LANES), jnp.float32)
    for t in range(tokens):
        ids = jnp.where(row == t, ids_ref[t].astype(jnp.float32), ids)
    ids = ids.astype(jnp.bfloat16)
    for j in range(chips):
        out_ref[j, :, :wide] = act_ref[:, j * wide : (j + 1) * wide]
        out_ref[j, :, wide : wide + units] = grads_ref[...]
        out_ref[j, :, wide + units :] = ids


def parcels_of(chips, activations, out_grads, query_ids):
    tokens, units = out_grads.shape
    wide = activations.shape[1] // chips
    return pl.pallas_call(
        parcel_kernel,
        out_shape=jax.ShapeDtypeStruct((chips, tokens, wide + units + LANES), jnp.bfloat16),
        in_specs=[
            pl.BlockSpec(memory_space=pltpu.SMEM),
            pl.BlockSpec(activations.shape, lambda: (0, 0)),
            pl.BlockSpec(out_grads.shape, lambda: (0, 0)),
        ],
        out_specs=pl.BlockSpec((chips, tokens, wide + units + LANES), lambda: (0, 0, 0)),
        compiler_params=pltpu.CompilerParams(vmem_limit_bytes=8 << 20),
        name="parcels",
    )(query_ids, *(pltpu.with_memory_space_constraint(v, pltpu.HBM) for v in (activations, out_grads)))


def ring_of(nz):
    return [0] + list(range(1, nz, 2)) + [z for z in range(nz - 1, 0, -1) if z % 2 == 0]


def streamed(shape, activations, out_grads, query_ids, act_basis, grad_basis, eigenvalues):
    ng, nz, ny, nc = shape
    count, order, _ = act_basis.shape
    width = count * order
    tokens = activations.shape[0]
    chips = nz * ny
    units = grad_basis.shape[0]

    def enc(g, z, y, c):
        return ((g * nz + z) * ny + y) * nc + c

    every = [
        (g, z, y, c) for g in range(ng) for z in range(nz) for y in range(ny) for c in range(nc)
    ]
    order_z = ring_of(nz)
    follow = {z: order_z[(i + 1) % nz] for i, z in enumerate(order_z)}
    before = {v: k for k, v in follow.items()}
    perm_core = [(enc(g, z, y, c), enc(g, z, y, 1 - c)) for g, z, y, c in every]
    perm_y = [(enc(g, z, y, c), enc(g, z, 1 - y, c)) for g, z, y, c in every]
    perm_z = [(enc(g, z, y, c), enc(g, follow[z], y, c)) for g, z, y, c in every]
    perm_zr = [(t, s) for s, t in perm_z]
    move = lambda v, p: lax.ppermute(v, AXES, p)

    where = jnp.stack([lax.axis_index(a) for a in AXES[1:]]).astype(jnp.int32)

    parcels = parcels_of(chips, activations, out_grads, query_ids)
    got = lax.all_to_all(parcels, ("z", "y"), split_axis=0, concat_axis=0, tiled=True)
    got = got.reshape(chips * tokens, nc * width + units + LANES)
    swapped = move(got, perm_core)

    along = [grad_basis] + [None] * (nz - 1)
    for k in range(1, nz // 2 + 1):
        along[k] = move(along[k - 1], perm_z)
        if nz - k > k:
            along[nz - k] = move(along[(nz - k + 1) % nz], perm_zr)
    levels = []
    for k in range(nz):
        across = move(along[k], perm_y)
        far = move(along[k], perm_core)
        far_across = move(across, perm_core)
        levels.append((along[k], across, far, far_across))

    dense = block_diagonal(where, act_basis)
    sel, og = tokens_of(order, where, got, swapped, dense, units)
    sources, level_z = [], list(range(nz))
    for _ in range(nz):
        sources.append(tuple(level_z))
        level_z = [before[v] for v in level_z]
    slots = nz // 2
    blocks = units // ROWS
    cut = blocks // 2

    def backs(ks):
        rb = None
        for slot, k in enumerate(ks):
            rb = back_of(
                order, sources[k], slot, slots, where, og, sel, dense, levels[k], eigenvalues, rb
            )
        return rb, [b for k in ks for b in levels[k]]

    rb, bases = backs(range(slots))
    acc = product_of(rb, bases, None, 0, cut, None)
    acc = product_of(rb, bases, None, cut, blocks - cut, acc)
    rb, bases = backs(range(slots, nz))
    return product_of(rb, bases, acc, 0, blocks // 2, None)


def plain(activations, out_grads, query_ids, act_basis, grad_basis, eigenvalues):
    local_blocks, block_order = act_basis.shape[:2]
    out_units = grad_basis.shape[0]
    columns = lax.all_to_all(activations, AXES[1:], split_axis=1, concat_axis=0, tiled=True)
    all_tokens = columns.shape[0]
    local_width = local_blocks * block_order
    rotated_act = jnp.einsum(
        "tbi,bik->tbk",
        columns.reshape(all_tokens, local_blocks, block_order),
        act_basis,
        preferred_element_type=jnp.float32,
    )
    rotated_act = rotated_act.astype(jnp.bfloat16).reshape(all_tokens, local_width)
    full_basis = lax.all_gather(grad_basis, AXES[1:], axis=1, tiled=True)
    own_rotated = jnp.dot(out_grads, full_basis, preferred_element_type=jnp.float32).astype(
        jnp.bfloat16
    )
    rotated_grad = lax.all_gather(own_rotated, AXES[1:], axis=0, tiled=True)
    token_query = lax.all_gather(query_ids, AXES[1:], axis=0, tiled=True)
    selector = (token_query[:, None] == jnp.arange(QUERIES, dtype=jnp.int32)[None, :]).astype(
        jnp.bfloat16
    )
    results = []
    for q in range(QUERIES):
        moments = lax.dot_general(
            rotated_grad,
            rotated_act * selector[:, q : q + 1],
            (((0,), (0,)), ((), ())),
            preferred_element_type=jnp.float32,
        )
        scaled = (moments / eigenvalues).astype(jnp.bfloat16)
        back = jnp.einsum(
            "dbk,bik->dbi",
            scaled.reshape(out_units, local_blocks, block_order),
            act_basis,
            preferred_element_type=jnp.float32,
        )
        back = back.astype(jnp.bfloat16).reshape(out_units, local_width)
        results.append(
            jnp.dot(full_basis, back, preferred_element_type=jnp.float32).astype(jnp.bfloat16)
        )
    return jnp.stack(results, axis=0)


def solution(mesh):
    ng, ns = mesh.shape["groups"], mesh.shape["seq"]
    ny = nc = 2
    nz = ns // (ny * nc)
    shape = (ng, nz, ny, nc)
    fine = Mesh(mesh.devices.reshape(shape), AXES)
    seq = AXES[1:]

    def body(activations, out_grads, query_ids, act_basis, grad_basis, eigenvalues):
        shard = grad_basis.shape[1]
        width = act_basis.shape[0] * act_basis.shape[1]
        if shard % LANES or width % LANES or nz % 2 or grad_basis.shape[0] % (2 * ROWS):
            return plain(activations, out_grads, query_ids, act_basis, grad_basis, eigenvalues)
        return streamed(
            shape, activations, out_grads, query_ids, act_basis, grad_basis, eigenvalues
        )

    return jax.shard_map(
        body,
        mesh=fine,
        in_specs=(
            P(AXES, None),
            P(AXES, None),
            P(AXES),
            P(seq, None, None),
            P(None, seq),
            P(None, seq),
        ),
        out_specs=P("g", None, seq),
        check_vma=False,
    )
```
